128 devices in a mesh: inst: 4 (over z), tile: 32 (over y, x, core).
Axes of the slice: x: 4, y: 4, z: 4, core: 2. Of those that a mesh axis runs over, the one named last changes fastest.
Arguments:
- morph: bfloat16 [1024, 16384], P(None, ('inst', 'tile')), may hold values from -6 to 6
- psf_x: bfloat16 [4, 6, 17], P('inst'), may hold values from 0.0099487305 to 0.25
- psf_y: bfloat16 [4, 6, 17], P('inst'), may hold values from 0.0099487305 to 0.25
- offsets: int32 [4, 6], P('inst'), may hold values from -8 to 8, as said below
- ratios: int32 [4], P('inst'), may hold values from 2 to 4, as said below
- observed: float32 [4, 6, 512, 8192], P('inst', None, 'tile'), may hold values from -6 to 6
- pixel_mask: int32 [4, 6, 512, 8192], P('inst', None, 'tile'), may hold values 0 or 1
Outputs:
- gradient: float32 [1024, 16384], P(None, ('inst', 'tile'))
The draws below stay inside these ranges and needn't reach their ends.
Inputs may be any that keep to these rules, and one draw needn't show every extreme that they name: `offsets`: both 8 and -8 occur. `ratios`: each value is 2 or 4, each held by half of the groups.
All inputs are finite; a program needn't handle non-finite values. No bound on the sum of `pixel_mask` on one device may be relied on, other than what follows from the above.
Results may differ from the reference program's by a relative error of at most 0.0016.
Values may be sent and summed in bfloat16 or wider, within the bound.
A program may use at most 128 MiB of HBM per device.

```python
import math
import jax
import jax.numpy as jnp
from jax import lax

CW = 32
BANDS = 6
H = 8
OFF = 8
YB = 1024
YM = 128
GROUPS = 4
NX = 1024
NY = 16384


def draw_offsets(key, part):
    first_key, second_key = jax.random.split(jax.random.fold_in(key, 11))
    values = jax.random.randint(first_key, (GROUPS * BANDS,), -OFF, OFF + 1)
    shuffled = jax.random.permutation(second_key, GROUPS * BANDS)
    values = values.at[shuffled[0]].set(OFF).at[shuffled[1]].set(-OFF)
    return values.reshape(GROUPS, BANDS).astype(jnp.int32)


def draw_ratios(key, part):
    shuffled = jax.random.permutation(jax.random.fold_in(key, 23), GROUPS)
    return jnp.where(shuffled < GROUPS // 2, 2, 4).astype(jnp.int32)


def plant(drawn, rng, least, largest):
    longest = drawn.shape.index(max(drawn.shape))
    spots = []
    for shift in (0, 1):
        where = [jax.random.randint(jax.random.fold_in(rng, axis), (), 0, length) for axis, length in enumerate(drawn.shape)]
        where[longest] = (where[longest] + shift) % drawn.shape[longest]
        spots.append(tuple(where))
    return drawn.at[spots[0]].set(least).at[spots[1]].set(largest)


def shard_levels(rng, dims, cuts, least, largest):
    gain, own = 1.0, jax.random.fold_in(rng, 6)
    for position, shards_of in cuts:
        heights = jnp.exp(jax.random.uniform(jax.random.fold_in(own, position), (shards_of,), jnp.float32, least / len(cuts), largest / len(cuts)))
        gain = gain * jnp.repeat(heights, dims[position] // shards_of).reshape([-1 if axis == position else 1 for axis in range(len(dims))])
    return gain


def scatter_about(own_key, shape, scale, limit, cuts=(), held_as=jnp.bfloat16):
    values = scale * jax.random.normal(own_key, shape, jnp.float32)
    if cuts:
        values = values * shard_levels(own_key, shape, cuts, -0.22, 0.18)
    return jnp.clip(values, -limit, limit).astype(held_as)


def setup_inputs(seed: int = 0) -> dict:
    keys = jax.random.split(jax.random.key(seed), 8)
    morph = scatter_about(keys[0], (NX, NY), 1.0, 6.0, ((1, 128),))
    psf_x = jnp.clip(jnp.exp(math.log(0.25) - 3.224016 * jax.random.uniform(keys[1], (GROUPS, BANDS, 2 * H + 1), jnp.float32) ** shard_levels(keys[1], (GROUPS, BANDS, 2 * H + 1), ((0, 4),), -0.2, 0.2)), 0.0099487305, 0.25).astype(jnp.bfloat16)
    psf_y = jnp.clip(jnp.exp(math.log(0.25) - 3.224016 * jax.random.uniform(keys[2], (GROUPS, BANDS, 2 * H + 1), jnp.float32) ** shard_levels(keys[2], (GROUPS, BANDS, 2 * H + 1), ((0, 4),), -0.2, 0.2)), 0.0099487305, 0.25).astype(jnp.bfloat16)
    offsets = draw_offsets(jax.random.fold_in(keys[7], 71), 0)
    ratios = draw_ratios(jax.random.fold_in(keys[7], 71), 0)
    observed = scatter_about(keys[5], (GROUPS, BANDS, NX // 2, NY // 2), 1.0, 6.0, ((0, 4), (2, 32)), jnp.float32)
    pixel_mask = plant((jax.random.randint(keys[6], (GROUPS, BANDS, NX // 2, NY // 2), 0, 10) < 9).astype(jnp.int32), jax.random.fold_in(keys[6], 1), 0, 1)
    return {"morph": morph, "psf_x": psf_x, "psf_y": psf_y, "offsets": offsets, "ratios": ratios, "observed": observed, "pixel_mask": pixel_mask}


def pair_mean(values, axis, coarser):
    count = values.shape[axis]
    halves = (lax.slice_in_dim(values, 0, count, 2, axis) + lax.slice_in_dim(values, 1, count, 2, axis)) * 0.5
    half_count = halves.shape[axis]
    quarters = (lax.slice_in_dim(halves, 0, half_count, 2, axis) + lax.slice_in_dim(halves, 1, half_count, 2, axis)) * 0.5
    quarters = jnp.concatenate([quarters, jnp.zeros_like(quarters)], axis=axis)
    return jnp.where(coarser, quarters, halves)


def reference(morph, psf_x, psf_y, offsets, ratios, observed, pixel_mask):
    rows_all, cols_all = morph.shape
    tile_count = rows_all // CW
    block_count = cols_all // YB
    combos = GROUPS * BANDS
    padded_x = jnp.pad(morph.astype(jnp.float32), ((H, H), (0, 0)))
    kern_all_x = psf_x.astype(jnp.float32).reshape(combos, 2 * H + 1)
    kern_all_y = psf_y.astype(jnp.float32).reshape(combos, 2 * H + 1)
    offset_all = offsets.reshape(combos)
    ratio_all = jnp.repeat(ratios, BANDS)
    observed_all = observed.reshape(combos, rows_all // 2, cols_all // 2)
    mask_all = pixel_mask.reshape(combos, rows_all // 2, cols_all // 2)
    coarse_pos = jnp.arange(rows_all // 2, dtype=jnp.int32) % (CW // 2)
    column_pos = jnp.arange(cols_all // 2, dtype=jnp.int32) % (YB // 2)

    def one_combo(running, combo_item):
        kern_x, kern_y, offset_now, ratio_now, observed_now, mask_now = combo_item
        coarser = ratio_now == 4
        blurred = jnp.zeros((rows_all, cols_all), jnp.float32)
        for tap_num in range(2 * H + 1):
            blurred = blurred + kern_x[tap_num] * padded_x[tap_num:tap_num + rows_all]
        tiles = blurred.reshape(tile_count, CW, cols_all)
        coarse = pair_mean(tiles, 1, coarser).reshape(rows_all // 2, cols_all).astype(jnp.bfloat16)
        coarse = lax.optimization_barrier(coarse).astype(jnp.float32)
        coarse_pad = jnp.pad(coarse, ((0, 0), (YM, YM)))
        smooth = jnp.zeros((rows_all // 2, cols_all), jnp.float32)
        for tap_num in range(2 * H + 1):
            start = (YM + tap_num - H + offset_now).astype(jnp.int32)
            smooth = smooth + kern_y[tap_num] * lax.dynamic_slice_in_dim(coarse_pad, start, cols_all, 1)
        model_sky = pair_mean(smooth.reshape(rows_all // 2, block_count, YB), 2, coarser)
        model_sky = model_sky.reshape(rows_all // 2, cols_all // 2)
        live_pixels = (coarse_pos < CW // ratio_now)[:, None] & (column_pos < YB // ratio_now)[None, :] & (mask_now == 1)
        misfit = jnp.where(live_pixels, model_sky - observed_now, 0.0)
        misfit_blocks = misfit.reshape(rows_all // 2, block_count, YB // 2)
        doubled = jnp.repeat(misfit_blocks, 2, axis=2) * 0.5
        quadrupled = jnp.repeat(misfit_blocks[:, :, :YB // 4], 4, axis=2) * 0.25
        spread = jnp.where(coarser, quadrupled, doubled).reshape(rows_all // 2, cols_all).astype(jnp.bfloat16)
        spread = lax.optimization_barrier(spread).astype(jnp.float32)
        spread_pad = jnp.pad(spread, ((0, 0), (YM, YM)))
        spread_back = jnp.zeros((rows_all // 2, cols_all), jnp.float32)
        for tap_num in range(2 * H + 1):
            start = (YM + H - tap_num - offset_now).astype(jnp.int32)
            spread_back = spread_back + kern_y[tap_num] * lax.dynamic_slice_in_dim(spread_pad, start, cols_all, 1)
        back_tiles = spread_back.reshape(tile_count, CW // 2, cols_all)
        doubled_x = jnp.repeat(back_tiles, 2, axis=1) * 0.5
        quadrupled_x = jnp.repeat(back_tiles[:, :CW // 4], 4, axis=1) * 0.25
        upsampled = jnp.where(coarser, quadrupled_x, doubled_x).reshape(rows_all, cols_all)
        padded_back = jnp.pad(upsampled, ((H, H), (0, 0)))
        for tap_num in range(2 * H + 1):
            begin = 2 * H - tap_num
            running = running + kern_x[tap_num] * padded_back[begin:begin + rows_all]
        return running, None

    running = jnp.zeros((rows_all, cols_all), jnp.float32)
    running, _ = lax.scan(one_combo, running, (kern_all_x, kern_all_y, offset_all, ratio_all, observed_all, mask_all))
    return running
```

```python
import functools
import jax
import jax.numpy as jnp
from jax import lax
from jax.experimental import pallas as pl
from jax.experimental.pallas import tpu as pltpu
from jax.sharding import PartitionSpec as P

MESH = pl.DeviceIdType.MESH
F32 = jnp.float32
BF16 = jnp.bfloat16
Q = 32700.0


def tables(psf_x, psf_y, offsets, ratio):
    r = ratio.astype(jnp.int32)
    inv = 1.0 / r.astype(F32)
    q = jnp.arange(16)[:, None]
    u = jnp.arange(48)[None, :]
    a = jnp.zeros((6, 16, 48), F32)
    for s in range(4):
        for d in range(17):
            hit = (u - q * r - s == d) & (s < r) & (q < 32 // r)
            a = a + jnp.where(hit[None], psf_x[:, d][:, None, None], 0.0)
    a = (a * inv).reshape(96, 48)
    k = jnp.arange(128)[None, :]
    prof = jnp.zeros((6, 128), F32)
    for s in range(4):
        for d in range(17):
            hit = (k - 64 - s + 8 - offsets[:, None] == d) & (s < r)
            prof = prof + jnp.where(hit, psf_y[:, d][:, None], 0.0)
    prof = prof * inv
    return a, a.T, prof


def gather_kernel(morph_ref, strip_ref, pad, send_sem, recv_sem, own_sem):
    mi = lax.axis_index("inst")
    mt = lax.axis_index("tile")
    me = mi * 32 + mt
    barrier = pltpu.get_barrier_semaphore()

    @pl.loop(1, 128)
    def _(j):
        to = lax.rem(me + j, 128)
        pl.semaphore_signal(barrier, inc=1, device_id=(to // 32, lax.rem(to, 32)), device_id_type=MESH)

    pad[...] = jnp.zeros_like(pad)
    pad[pl.ds(8, 1024), :] = morph_ref[...]
    pl.semaphore_wait(barrier, 127)
    mine = strip_ref.at[:, pl.ds(pl.multiple_of(me * 128, 128), 128)]

    @pl.loop(1, 128)
    def _(j):
        to = lax.rem(me + j, 128)
        tt = lax.rem(to, 32)
        pltpu.make_async_remote_copy(
            src_ref=pad.at[pl.ds(pl.multiple_of(tt * 32, 32), 48), :],
            dst_ref=mine,
            send_sem=send_sem,
            recv_sem=recv_sem,
            device_id=(to // 32, tt),
            device_id_type=MESH,
        ).start()

    own = pltpu.make_async_copy(pad.at[pl.ds(pl.multiple_of(mt * 32, 32), 48), :], mine, own_sem)
    own.start()
    own.wait()
    rest = strip_ref.at[:, pl.ds(0, 127 * 128)]
    pltpu.make_async_copy(rest, rest, send_sem).wait()
    pltpu.make_async_copy(rest, rest, recv_sem).wait()


def gather(morph):
    return pl.pallas_call(
        gather_kernel,
        out_shape=jax.ShapeDtypeStruct((48, 16384), BF16),
        in_specs=[pl.BlockSpec(memory_space=pltpu.VMEM)],
        out_specs=pl.BlockSpec(memory_space=pltpu.VMEM),
        scratch_shapes=[
            pltpu.VMEM((1040, 128), BF16),
            pltpu.SemaphoreType.DMA,
            pltpu.SemaphoreType.DMA,
            pltpu.SemaphoreType.DMA,
        ],
        compiler_params=pltpu.CompilerParams(collective_id=0, has_side_effects=True, vmem_limit_bytes=16 << 20),
    )(morph)


def split(x):
    hi = x.astype(BF16)
    return hi, (x - hi.astype(F32)).astype(BF16)


def fit_kernel(
    ratio_ref, x_ref, obs_hbm, mask_hbm, a_ref, at_ref, prof_ref, out_ref,
    obs, mask, wc, vh, vl, c3, m3, t3, sem,
):
    r = ratio_ref[0]
    load_obs = pltpu.make_async_copy(obs_hbm, obs, sem.at[0])
    load_mask = pltpu.make_async_copy(mask_hbm, mask, sem.at[1])
    load_obs.start()
    load_mask.start()

    def pick(index, b):
        clipped = jnp.clip(index + 64, 0, 127)
        row = jnp.broadcast_to(prof_ref[pl.ds(b, 1), :], clipped.shape)
        return jnp.take_along_axis(row, clipped, axis=1)

    @pl.loop(0, 48)
    def _(g):
        base = pl.multiple_of(g * 16, 16)
        u = base + lax.broadcasted_iota(jnp.int32, (16, 128), 0)
        c = lax.broadcasted_iota(jnp.int32, (16, 128), 1)
        index = u - 128 - r * c
        for b in range(6):
            hi, lo = split(pick(index, b))
            wc[b, pl.ds(base, 16), pl.ds(0, 128)] = hi
            wc[b, pl.ds(base, 16), pl.ds(128, 128)] = lo

    @pl.loop(0, 32)
    def _(g):
        base = pl.multiple_of(g * 16, 16)
        for n in range(4):
            c = base + lax.broadcasted_iota(jnp.int32, (16, 128), 0)
            f = n * 128 + lax.broadcasted_iota(jnp.int32, (16, 128), 1)
            index = f - r * (c - 128)
            for b in range(6):
                hi, lo = split(pick(index, b))
                vh[b, pl.ds(base, 16), pl.ds(n * 128, 128)] = hi
                vl[b, pl.ds(base, 16), pl.ds(n * 128, 128)] = lo

    a_hi, a_lo = split(a_ref[...])
    a_both = jnp.concatenate([a_hi, a_lo], axis=1)
    at_hi, at_lo = split(at_ref[...])
    at_both = jnp.concatenate(
        [jnp.concatenate([at_hi, at_hi], axis=1), jnp.concatenate([at_lo, at_lo], axis=1)], axis=0
    )
    zero = jnp.zeros((96, 128), BF16)
    for n in (0, 129, 130, 131):
        c3[n] = zero
    for n in (0, 65):
        m3[n] = zero

    @pl.loop(0, 64)
    def _(n):
        x = x_ref[:, pl.ds(pl.multiple_of(n * 256, 256), 256)]
        c = jnp.dot(a_both, jnp.concatenate([x, x], axis=0), preferred_element_type=F32).astype(BF16)
        c3[1 + 2 * n] = c[:, :128]
        c3[2 + 2 * n] = c[:, 128:]

    load_obs.wait()
    load_mask.wait()
    q = lax.broadcasted_iota(jnp.int32, (16, 128), 0)
    row_live = q * r < 32

    @pl.loop(0, 24)
    def _(step):
        b = step // 4
        g = lax.rem(step, 4)
        rows = pl.ds(pl.multiple_of(b * 16, 16), 16)
        parts = []
        for j in range(16):
            first = jnp.minimum(r * (g * 16 + j), 126)
            parts.append(jnp.concatenate([c3[first + s, rows, :] for s in range(6)], axis=1))
        both = jnp.dot(jnp.concatenate(parts, axis=0), wc[b], preferred_element_type=F32)
        model = both[:, :128] + both[:, 128:]
        for j in range(16):
            jj = g * 16 + j
            at = jnp.where(r == 2, jj * 128, jnp.minimum((jj // 2) * 512 + lax.rem(jj, 2) * 128, 8064))
            cols = pl.ds(pl.multiple_of(at, 128), 128)
            live = (mask[b, :, cols] == 1) & row_live & (r * jj < 128)
            misfit = jnp.where(live, model[j * 16 : (j + 1) * 16] - obs[b, :, cols], 0.0)
            m3[1 + jj, rows, :] = misfit.astype(BF16)

    per = 4 // r

    @pl.loop(0, 24)
    def _(step):
        b = step // 4
        g = lax.rem(step, 4)
        rows = pl.ds(pl.multiple_of(b * 16, 16), 16)
        low = pl.ds(pl.multiple_of(96 + b * 16, 16), 16)
        parts = []
        for j in range(8):
            first = per * (g * 8 + j)
            parts.append(jnp.concatenate([m3[first + s, rows, :] for s in range(4)], axis=1))
        lhs = jnp.concatenate(parts, axis=0)
        back = jnp.dot(lhs, vh[b], preferred_element_type=F32) + jnp.dot(lhs, vl[b], preferred_element_type=F32)
        hi, lo = split(back)
        for j in range(8):
            for s in range(4):
                n = (g * 8 + j) * 4 + s
                t3[n, rows, :] = hi[j * 16 : (j + 1) * 16, s * 128 : (s + 1) * 128]
                t3[n, low, :] = lo[j * 16 : (j + 1) * 16, s * 128 : (s + 1) * 128]

    @pl.loop(0, 64)
    def _(n):
        t = jnp.concatenate([t3[2 * n], t3[2 * n + 1]], axis=1)
        both = jnp.dot(at_both, t, preferred_element_type=F32)
        grad = both[:48] + both[48:]
        for h in range(2):
            part = grad[:, h * 128 : (h + 1) * 128]
            top = jnp.max(jnp.abs(part), axis=0, keepdims=True)
            power = jnp.ceil(jnp.log2(jnp.maximum(top, 1e-37)) * 8.0)
            scaled = part * jnp.exp2(power * -0.125)
            out_ref[2 * n + h, pl.ds(0, 48), :] = jnp.round(scaled * Q).astype(jnp.int32).astype(jnp.int16)
            out_ref[2 * n + h, pl.ds(48, 8), :] = jnp.broadcast_to(power, (8, 128)).astype(jnp.int32).astype(jnp.int16)


def fit(ratio, strip, observed, pixel_mask, a, at, prof):
    vmem = pl.BlockSpec(memory_space=pltpu.VMEM)
    hbm = pl.BlockSpec(memory_space=pl.ANY)
    return pl.pallas_call(
        fit_kernel,
        out_shape=jax.ShapeDtypeStruct((128, 56, 128), jnp.int16),
        in_specs=[pl.BlockSpec(memory_space=pltpu.SMEM), vmem, hbm, hbm, vmem, vmem, vmem],
        out_specs=vmem,
        scratch_shapes=[
            pltpu.VMEM((6, 16, 8192), F32),
            pltpu.VMEM((6, 16, 8192), jnp.int32),
            pltpu.VMEM((6, 768, 256), BF16),
            pltpu.VMEM((6, 512, 512), BF16),
            pltpu.VMEM((6, 512, 512), BF16),
            pltpu.VMEM((132, 96, 128), BF16),
            pltpu.VMEM((66, 96, 128), BF16),
            pltpu.VMEM((128, 192, 128), BF16),
            pltpu.SemaphoreType.DMA((2,)),
        ],
        compiler_params=pltpu.CompilerParams(vmem_limit_bytes=48 << 20),
    )(ratio, strip, observed, pixel_mask, a, at, prof)


def scatter_kernel(grad_ref, out_ref, got, send_sem, recv_sem, own_sem):
    mi = lax.axis_index("inst")
    mt = lax.axis_index("tile")
    me = mi * 32 + mt
    barrier = pltpu.get_barrier_semaphore()

    @pl.loop(1, 128)
    def _(j):
        to = lax.rem(me + j, 128)
        pl.semaphore_signal(barrier, inc=1, device_id=(to // 32, lax.rem(to, 32)), device_id_type=MESH)

    pl.semaphore_wait(barrier, 127)

    @pl.loop(1, 128)
    def _(j):
        to = lax.rem(me + j, 128)
        pltpu.make_async_remote_copy(
            src_ref=grad_ref.at[to],
            dst_ref=got.at[me],
            send_sem=send_sem,
            recv_sem=recv_sem,
            device_id=(to // 32, lax.rem(to, 32)),
            device_id_type=MESH,
        ).start()

    own = pltpu.make_async_copy(grad_ref.at[me], got.at[me], own_sem)
    own.start()
    own.wait()
    rest = got.at[pl.ds(0, 127)]
    pltpu.make_async_copy(rest, rest, send_sem).wait()
    pltpu.make_async_copy(rest, rest, recv_sem).wait()

    def piece(dev, first, count):
        scale = jnp.exp2(got[dev, pl.ds(48, 8), :].astype(jnp.int32).astype(F32) * 0.125) * (1.0 / Q)
        value = got[dev, pl.ds(first, count), :].astype(jnp.int32).astype(F32)
        return value * jnp.broadcast_to(scale[:1], (count, 128))

    @pl.loop(0, 32)
    def _(t):
        base = pl.multiple_of(t * 32, 32)
        above = jnp.where(t > 0, 1.0, 0.0)
        below = jnp.where(t < 31, 1.0, 0.0)
        up = jnp.maximum(t - 1, 0)
        down = jnp.minimum(t + 1, 31)
        total = piece(t, 8, 32)
        head = piece(up, 40, 8)
        tail = piece(down, 0, 8)
        for i in range(1, 4):
            total = total + piece(i * 32 + t, 8, 32)
            head = head + piece(i * 32 + up, 40, 8)
            tail = tail + piece(i * 32 + down, 0, 8)
        out_ref[pl.ds(base, 8), :] = total[:8] + head * above
        out_ref[pl.ds(base + 8, 16), :] = total[8:24]
        out_ref[pl.ds(base + 24, 8), :] = total[24:] + tail * below


def scatter(grad):
    return pl.pallas_call(
        scatter_kernel,
        out_shape=jax.ShapeDtypeStruct((1024, 128), F32),
        in_specs=[pl.BlockSpec(memory_space=pltpu.VMEM)],
        out_specs=pl.BlockSpec(memory_space=pltpu.VMEM),
        scratch_shapes=[
            pltpu.VMEM((128, 56, 128), jnp.int16),
            pltpu.SemaphoreType.DMA,
            pltpu.SemaphoreType.DMA,
            pltpu.SemaphoreType.DMA,
        ],
        compiler_params=pltpu.CompilerParams(collective_id=1, has_side_effects=True, vmem_limit_bytes=16 << 20),
    )(grad)


def per_device(morph, psf_x, psf_y, offsets, ratios, observed, pixel_mask):
    a, at, prof = tables(psf_x[0].astype(F32), psf_y[0].astype(F32), offsets[0], ratios[0])
    strip = gather(morph)
    grad = fit(ratios, strip, observed[0], pixel_mask[0], a, at, prof)
    return scatter(grad)


def solution(mesh):
    return jax.shard_map(
        per_device,
        mesh=mesh,
        in_specs=(
            P(None, ("inst", "tile")),
            P("inst", None, None),
            P("inst", None, None),
            P("inst", None),
            P("inst"),
            P("inst", None, "tile", None),
            P("inst", None, "tile", None),
        ),
        out_specs=P(None, ("inst", "tile")),
        check_vma=False,
    )
```
